32 devices in a mesh: cells: 8 (over z, x), genes: 4 (over y, core).
Axes of the slice: x: 2, y: 2, z: 4, core: 2. Of those that a mesh axis runs over, the one named last changes fastest.
Arguments:
- expression: bfloat16 [32768, 4096], P('cells', 'genes'), may hold values from -200 to 200
- labels: int32 [32768], P('cells'), may hold values from 0 to 199, as said below
- loadings: bfloat16 [4096, 50], P('genes'), may hold values from -0.09375 to 0.09375
Outputs:
- adjusted: bfloat16 [32768, 4096], P('cells', 'genes')
- scores: float32 [32768, 50], P('cells')
The draws below stay inside these ranges and needn't reach their ends.
Inputs may be any that keep to these rules, and one draw needn't show every extreme that they name: `labels`: every batch has two or more cells.
All inputs are finite; a program needn't handle non-finite values.
Results may differ from the reference program's by a relative error of at most 0.0029.
Values sent between devices are 32-bit elements; how exact they have to be, the bound alone decides.
A program may use at most 64 MiB of HBM per device.

```python
import math
import jax
import jax.numpy as jnp
from jax import lax

GENES = 4096
BATCHES = 200
COMPONENTS = 50
SWEEPS = 10
CELLS = 32768


def label_table(key):
    rare_count = BATCHES // 3
    common_count = BATCHES - rare_count
    rare_top = max(2, min(30, CELLS // (2 * BATCHES)))
    keys = jax.random.split(jax.random.fold_in(key, 11), 5)
    order = jax.random.permutation(keys[0], BATCHES).astype(jnp.int32)
    rare_ids = order[:rare_count]
    common_ids = order[rare_count:]
    rare_sizes = jax.random.randint(keys[1], (rare_count,), 2, rare_top + 1, dtype=jnp.int32)
    rare_ends = jnp.cumsum(rare_sizes).astype(jnp.int32)
    rare_total = rare_ends[rare_count - 1]
    position = jnp.arange(CELLS, dtype=jnp.int32)
    rare_slot = jnp.minimum(jnp.searchsorted(rare_ends, position, side='right').astype(jnp.int32), rare_count - 1)
    base_slot = jnp.clip((position - rare_total) // 2, 0, common_count - 1).astype(jnp.int32)
    pick_first = jax.random.randint(keys[2], (CELLS,), 0, common_count, dtype=jnp.int32)
    pick_second = jax.random.randint(keys[3], (CELLS,), 0, common_count, dtype=jnp.int32)
    extra_slot = jnp.minimum(pick_first, pick_second)
    ordered = jnp.where(position < rare_total, rare_ids[rare_slot], jnp.where(position < rare_total + 2 * common_count, common_ids[base_slot], common_ids[extra_slot]))
    shuffle = jax.random.permutation(keys[4], CELLS).astype(jnp.int32)
    return ordered[shuffle].astype(jnp.int32)


def draw_labels(key, part):
    return label_table(key)


def draw_expression(key, part):
    labels = label_table(key)
    keys = jax.random.split(jax.random.fold_in(key, 23), 6)
    gene_scale = jnp.exp(jax.random.uniform(keys[0], (GENES,), jnp.float32, 0.0, jnp.log(10.0)))
    noise = jnp.clip(jax.random.normal(keys[4], (CELLS, GENES), jnp.float32), -5.0, 5.0)
    ramp_low = 0.5
    ramp_high = 3.0
    width_low = 0.2
    width_high = 0.8
    position = jnp.arange(GENES, dtype=jnp.float32) / (GENES - 1.0)
    gene_ramp = ramp_low + (ramp_high - ramp_low) * position
    gene_width = width_low + (width_high - width_low) * position
    gene_mean = jax.random.uniform(keys[1], (GENES,), jnp.float32, -2.0, 2.0)
    batch_offset = jax.random.uniform(keys[5], (BATCHES,), jnp.float32, -1.0, 1.0)
    shift = 0.4 * gene_ramp[None, :] * (jnp.clip(jax.random.normal(keys[2], (BATCHES, GENES), jnp.float32), -4.0, 4.0) + batch_offset[:, None])
    batch_scale = jnp.exp(jax.random.uniform(keys[3], (BATCHES, GENES), jnp.float32, -1.0, 1.0) * gene_width[None, :])
    values = gene_mean[None, :] + gene_scale[None, :] * (shift[labels] + batch_scale[labels] * noise) / 3.0
    return values.astype(jnp.bfloat16)


def shard_levels(rng, shape, pieces, least, largest):
    level, own = 1.0, jax.random.fold_in(rng, 6)
    for dim, shards_of in pieces:
        steps = jnp.exp(jax.random.uniform(jax.random.fold_in(own, dim), (shards_of,), jnp.float32, least / len(pieces), largest / len(pieces)))
        level = level * jnp.repeat(steps, shape[dim] // shards_of).reshape([-1 if axis == dim else 1 for axis in range(len(shape))])
    return level


def gaussian(own_key, shape, width, limit, cuts=(), kind=jnp.bfloat16):
    loudness = shard_levels(own_key, shape, cuts, -0.22, 0.18) if cuts else 1.0
    result = jax.random.normal(own_key, shape, jnp.float32) * width * loudness
    return jnp.minimum(jnp.maximum(result, -limit), limit).astype(kind)


def setup_inputs(seed: int = 0) -> dict:
    key_of = jax.random.split(jax.random.key(seed), 4)
    expression = draw_expression(jax.random.fold_in(key_of[3], 71), 0)
    labels = draw_labels(jax.random.fold_in(key_of[3], 71), 0)
    loadings = gaussian(key_of[2], (GENES, COMPONENTS), GENES ** -0.5, 0.09375, ((0, 4),))
    return {"expression": expression, "labels": labels, "loadings": loadings}


def batch_moments(sum_one, sum_two, counts, total_cells):
    grand = lax.optimization_barrier(jnp.sum(sum_one, axis=0)) / total_cells
    within = sum_two - sum_one * sum_one / counts[:, None]
    pooled = lax.optimization_barrier(jnp.sum(within, axis=0)) / total_cells + 1e-06
    gene_sd = jnp.sqrt(pooled)
    gamma_hat = (sum_one / counts[:, None] - grand[None, :]) / gene_sd[None, :]
    delta_hat = within / ((counts[:, None] - 1.0) * pooled[None, :])
    return (grand, gene_sd, gamma_hat, delta_hat)

def shrink(gamma_hat, delta_hat, counts):
    gamma_bar = lax.optimization_barrier(jnp.sum(gamma_hat, axis=1)) / GENES
    tau_sq = (lax.optimization_barrier(jnp.sum(gamma_hat * gamma_hat, axis=1)) - GENES * gamma_bar * gamma_bar) / (GENES - 1)
    delta_mean = lax.optimization_barrier(jnp.sum(delta_hat, axis=1)) / GENES
    delta_var = (lax.optimization_barrier(jnp.sum(delta_hat * delta_hat, axis=1)) - GENES * delta_mean * delta_mean) / (GENES - 1) + 1e-06
    a_prior = (2.0 * delta_var + delta_mean * delta_mean) / delta_var
    b_prior = (delta_mean * delta_var + delta_mean ** 3) / delta_var
    weight = counts[:, None]

    def sweep(sweep_index, state):
        gamma_now, delta_now = state
        gamma_next = (weight * tau_sq[:, None] * gamma_hat + delta_now * gamma_bar[:, None]) / (weight * tau_sq[:, None] + delta_now)
        sum_sq = (weight - 1.0) * delta_hat + weight * (gamma_hat - gamma_next) ** 2
        delta_next = (0.5 * sum_sq + b_prior[:, None]) / (0.5 * weight + a_prior[:, None] - 1.0)
        return (gamma_next, delta_next)
    gamma_star, delta_star = lax.fori_loop(0, SWEEPS, sweep, (gamma_hat, delta_hat))
    return (gamma_star, 1.0 / jnp.sqrt(delta_star))

def reference(expression, labels, loadings):
    block_rows = math.gcd(CELLS, 4096)
    block_count = CELLS // block_rows
    indices = jnp.arange(block_count, dtype=jnp.int32)

    def accumulate(totals, block_index):
        start = block_index * block_rows
        values = lax.dynamic_slice_in_dim(expression, start, block_rows, 0).astype(jnp.float32)
        local_labels = lax.dynamic_slice_in_dim(labels, start, block_rows, 0)
        first = jax.ops.segment_sum(values, local_labels, BATCHES)
        second = jax.ops.segment_sum(values * values, local_labels, BATCHES)
        number = jax.ops.segment_sum(jnp.ones((block_rows,), jnp.float32), local_labels, BATCHES)
        return ((totals[0] + first, totals[1] + second, totals[2] + number), None)
    zeros_table = jnp.zeros((BATCHES, GENES), jnp.float32)
    (sum_one, sum_two, counts), unused = lax.scan(accumulate, (zeros_table, zeros_table, jnp.zeros((BATCHES,), jnp.float32)), indices)
    grand, gene_sd, gamma_hat, delta_hat = batch_moments(sum_one, sum_two, counts, CELLS)
    gamma_star, scale_star = shrink(gamma_hat, delta_hat, counts)

    def adjust(block_index):
        start = block_index * block_rows
        values = lax.dynamic_slice_in_dim(expression, start, block_rows, 0).astype(jnp.float32)
        local_labels = lax.dynamic_slice_in_dim(labels, start, block_rows, 0)
        shifted = (values - grand[None, :]) / gene_sd[None, :]
        standard = (shifted - gamma_star[local_labels]) * scale_star[local_labels]
        adjusted = (gene_sd[None, :] * standard + grand[None, :]).astype(jnp.bfloat16)
        standard_low = standard.astype(jnp.bfloat16)
        partial_value = jnp.dot(standard_low, loadings, preferred_element_type=jnp.float32)
        return (adjusted, partial_value)
    adjusted, scores = lax.map(adjust, indices)
    return (adjusted.reshape(CELLS, GENES), scores.reshape(CELLS, COMPONENTS))
```

```python
import functools
import math

import jax
import jax.numpy as jnp
from jax import lax
from jax.experimental import pallas as pl
from jax.experimental.pallas import tpu as pltpu
from jax.sharding import PartitionSpec as P

BATCHES = 200
SWEEPS = 10
PADDED = 256
VMEM_LIMIT = 56 * 1024 * 1024


def one_hot(labels_row):
    ids = lax.broadcasted_iota(jnp.int32, (PADDED, labels_row.shape[1]), 0)
    return (ids == labels_row).astype(jnp.float32).astype(jnp.bfloat16)


def moments_kernel(labels_ref, values_ref, out_ref, *, chunks, width):
    step = pl.program_id(0)

    @pl.when(step == 0)
    def _():
        out_ref[...] = jnp.zeros_like(out_ref)

    members = one_hot(labels_ref[...])
    values = values_ref[...]
    wide = values.astype(jnp.float32)
    square = wide * wide
    upper = square.astype(jnp.bfloat16)
    lower = (square - upper.astype(jnp.float32)).astype(jnp.bfloat16)
    dot = functools.partial(jnp.dot, preferred_element_type=jnp.float32)
    first = dot(members, values)[:BATCHES]
    second = (dot(members, upper) + dot(members, lower))[:BATCHES]
    ones = jnp.ones((8, members.shape[1]), jnp.bfloat16)
    number = lax.dot_general(
        ones, members, (((1,), (1,)), ((), ())), preferred_element_type=jnp.float32
    )
    for chunk in range(chunks):
        cols = slice(chunk * width, (chunk + 1) * width)
        out_ref[chunk, :BATCHES, :] += first[:, cols]
        out_ref[chunk, BATCHES : 2 * BATCHES, :] += second[:, cols]
        for row in range(-(-PADDED // width)):
            size = min(width, PADDED - row * width)
            at = 2 * BATCHES + row
            out_ref[chunk, at : at + 1, :size] += number[:1, row * width : row * width + size]


def adjust_kernel(
    labels_ref, values_ref, table_ref, loadings_ref, adjusted_ref, scores_ref,
    parts_ref, lines_ref, *, chunks, width
):
    gene_cols = chunks * width

    @pl.when(pl.program_id(0) == 0)
    def _():
        parts_ref[...] = jnp.zeros_like(parts_ref)
        for chunk in range(chunks):
            for kind in range(2):
                part = table_ref[chunk, kind * BATCHES : (kind + 1) * BATCHES, :]
                upper = part.astype(jnp.bfloat16)
                lower = (part - upper.astype(jnp.float32)).astype(jnp.bfloat16)
                at = 2 * kind * gene_cols + chunk * width
                parts_ref[:BATCHES, at : at + width] = upper
                parts_ref[:BATCHES, at + gene_cols : at + gene_cols + width] = lower
            lines_ref[0:3, chunk * width : (chunk + 1) * width] = table_ref[
                chunk, 2 * BATCHES : 2 * BATCHES + 3, :
            ]

    members = one_hot(labels_ref[...]).T
    dot = functools.partial(jnp.dot, preferred_element_type=jnp.float32)
    part = lambda k: parts_ref[:, k * gene_cols : (k + 1) * gene_cols]
    gamma = dot(members, part(0)) + dot(members, part(1))
    scale = dot(members, part(2)) + dot(members, part(3))
    grand, gene_sd, inverse_sd = lines_ref[0:1, :], lines_ref[1:2, :], lines_ref[2:3, :]
    shifted = (values_ref[...].astype(jnp.float32) - grand) * inverse_sd
    standard = (shifted - gamma) * scale
    adjusted_ref[...] = (gene_sd * standard + grand).astype(jnp.bfloat16)
    partial_value = dot(standard.astype(jnp.bfloat16), loadings_ref[...])
    scores_ref[...] = partial_value.T[: scores_ref.shape[0]]


def body(expression, labels, loadings):
    cell_rows, gene_cols = expression.shape
    components = loadings.shape[1]
    chunks = lax.axis_size("cells")
    width = gene_cols // chunks
    total_cells = cell_rows * chunks
    genes = gene_cols * lax.axis_size("genes")
    block = math.gcd(cell_rows, 512)
    steps = cell_rows // block
    count_rows = -(-PADDED // width)
    rows = -(-(2 * BATCHES + max(count_rows, 3)) // 8) * 8
    labels_row = labels.reshape(1, cell_rows)
    params = pltpu.CompilerParams(
        dimension_semantics=("arbitrary",), vmem_limit_bytes=VMEM_LIMIT
    )
    labels_spec = pl.BlockSpec((1, block), lambda i: (0, i))
    values_spec = pl.BlockSpec((block, gene_cols), lambda i: (i, 0))
    table_spec = pl.BlockSpec((chunks, rows, width), lambda i: (0, 0, 0))
    moments = pl.pallas_call(
        functools.partial(moments_kernel, chunks=chunks, width=width),
        grid=(steps,),
        in_specs=[labels_spec, values_spec],
        out_specs=table_spec,
        out_shape=jax.ShapeDtypeStruct((chunks, rows, width), jnp.float32),
        compiler_params=params,
        name="moments",
    )(labels_row, expression)
    mine = lax.psum_scatter(moments, "cells", scatter_dimension=0, tiled=True)[0]
    sum_one = mine[:BATCHES]
    sum_two = mine[BATCHES : 2 * BATCHES]
    counts = mine[2 * BATCHES : 2 * BATCHES + count_rows].reshape(-1)[:BATCHES]
    weight = counts[:, None]
    grand = jnp.sum(sum_one, axis=0) / total_cells
    within = sum_two - sum_one * sum_one / weight
    pooled = jnp.sum(within, axis=0) / total_cells + 1e-06
    gene_sd = jnp.sqrt(pooled)
    gamma_hat = (sum_one / weight - grand[None, :]) / gene_sd[None, :]
    delta_hat = within / ((weight - 1.0) * pooled[None, :])
    local = jnp.stack(
        [
            jnp.sum(gamma_hat, axis=1),
            jnp.sum(gamma_hat * gamma_hat, axis=1),
            jnp.sum(delta_hat, axis=1),
            jnp.sum(delta_hat * delta_hat, axis=1),
        ]
    )
    spread = lax.psum(local, ("cells", "genes"))
    gamma_bar = spread[0] / genes
    tau_sq = (spread[1] - genes * gamma_bar * gamma_bar) / (genes - 1)
    delta_mean = spread[2] / genes
    delta_var = (spread[3] - genes * delta_mean * delta_mean) / (genes - 1) + 1e-06
    a_prior = (2.0 * delta_var + delta_mean * delta_mean) / delta_var
    b_prior = (delta_mean * delta_var + delta_mean**3) / delta_var
    pull = (counts * tau_sq)[:, None]
    bar = gamma_bar[:, None]
    prior = b_prior[:, None]
    inverse = (1.0 / (0.5 * counts + a_prior - 1.0))[:, None]
    gamma, delta = gamma_hat, delta_hat
    for _ in range(SWEEPS):
        gamma = (pull * gamma_hat + delta * bar) / (pull + delta)
        sum_sq = (weight - 1.0) * delta_hat + weight * (gamma_hat - gamma) ** 2
        delta = (0.5 * sum_sq + prior) * inverse
    scale = 1.0 / jnp.sqrt(delta)
    table = jnp.concatenate(
        [
            gamma,
            scale,
            grand[None, :],
            gene_sd[None, :],
            (1.0 / gene_sd)[None, :],
            jnp.zeros((rows - 2 * BATCHES - 3, width), jnp.float32),
        ],
        axis=0,
    )
    tables = lax.all_gather(table[None], "cells", axis=0, tiled=True)
    lanes = -(-components // 128) * 128
    padded_loadings = jnp.pad(loadings, ((0, 0), (0, lanes - components)))
    adjusted, partial_value = pl.pallas_call(
        functools.partial(adjust_kernel, chunks=chunks, width=width),
        grid=(steps,),
        in_specs=[
            labels_spec,
            values_spec,
            table_spec,
            pl.BlockSpec((gene_cols, lanes), lambda i: (0, 0)),
        ],
        out_specs=[values_spec, pl.BlockSpec((components, block), lambda i: (0, i))],
        out_shape=[
            jax.ShapeDtypeStruct((cell_rows, gene_cols), jnp.bfloat16),
            jax.ShapeDtypeStruct((components, cell_rows), jnp.float32),
        ],
        scratch_shapes=[
            pltpu.VMEM((PADDED, 4 * gene_cols), jnp.bfloat16),
            pltpu.VMEM((8, gene_cols), jnp.float32),
        ],
        compiler_params=params,
        name="adjust",
    )(labels_row, expression, tables, padded_loadings)
    return (adjusted, lax.psum(partial_value, "genes").T)


def solution(mesh):
    placed = (P("cells", "genes"), P("cells"), P("genes", None))
    return jax.shard_map(
        body,
        mesh=mesh,
        in_specs=placed,
        out_specs=(P("cells", "genes"), P("cells", None)),
        check_vma=False,
    )
```
